128 devices in a mesh: frame: 8 (over y, core), module: 16 (over z, x).
Axes of the slice: x: 4, y: 4, z: 4, core: 2. Of those that a mesh axis runs over, the one named last changes fastest.
Arguments:
- frames: bfloat16 [2048, 196608], P('frame', 'module'), may hold values from -6 to 6
- weights: bfloat16 [1536, 512, 128], P('module'), may hold values from 0 to 0.25
- monitor: float32 [2048], P('frame'), may hold values from 0.5 to 2
- coverage: int32 [16, 96], replicated, may hold values from 0 to 255, as said below
- block_slot: int32 [16, 96], P('module'), may hold values from 0 to 95, each once within a row
- angle_index: int32 [4], replicated, may hold values from 0 to 179
Outputs:
- slices: bfloat16 [2, 8, 16, 128, 8192], P(None, 'frame', 'module')
The draws below stay inside these ranges and needn't reach their ends.
Inputs may be any that keep to these rules, and one draw needn't show every extreme that they name: `coverage`: row m holds 96 consecutive tile numbers s, s + 1, ... taken modulo 256, in order, for a start s of its own. `block_slot`: each row is a permutation.
All inputs are finite; a program needn't handle non-finite values.
Results may differ from the reference program's by a relative error of at most 0.0055.
Values sent between devices are 32-bit elements; how exact they have to be, the bound alone decides.
No kernel may reach another device: no remote copies, remote signals or barrier semaphores. Data moves between devices by JAX's collectives and lax.ppermute only.
A program may use at most 192 MiB of HBM per device.

```python
import math
import jax
import jax.numpy as jnp
from jax import lax

TILE = 128
TRANS = 512
TPM = 96
SPLITS = 4
PB = 512
ASTEPS = 180
ROWS = 16
NTILE = 256
PIX = 12288
MODULES = 16
GROUPS = 8
FRAMES = 2048
ANGLES = 4
QT = 2


def draw_coverage(key, part):
    start_key, pick_key, wrap_key = jax.random.split(key, 3)
    starts = jax.random.randint(start_key, (MODULES,), 0, NTILE)
    chosen = jax.random.randint(pick_key, (), 0, MODULES)
    wrapped = NTILE - 1 - jax.random.randint(wrap_key, (), 0, TPM - 1)
    starts = jnp.where(jnp.arange(MODULES) == chosen, wrapped, starts)
    return ((starts[:, None] + jnp.arange(TPM)[None, :]) % NTILE).astype(jnp.int32)


def place_ends(array, own_key, low, high):
    longest = array.shape.index(max(array.shape))
    spots = []
    for shift in (0, 1):
        where = [jax.random.randint(jax.random.fold_in(own_key, axis), (), 0, length) for axis, length in enumerate(array.shape)]
        where[longest] = (where[longest] + shift) % array.shape[longest]
        spots.append(tuple(where))
    return array.at[spots[0]].set(low).at[spots[1]].set(high)


def level_of(stream_key, extent, cuts, least, largest):
    level, own = 1.0, jax.random.fold_in(stream_key, 6)
    for dim, blocks in cuts:
        heights = jnp.exp(jax.random.uniform(jax.random.fold_in(own, dim), (blocks,), jnp.float32, least / len(cuts), largest / len(cuts)))
        level = level * jnp.repeat(heights, extent[dim] // blocks).reshape([-1 if axis == dim else 1 for axis in range(len(extent))])
    return level


def centred(key, shape, spread, limit, pieces=(), held_as=jnp.bfloat16):
    entries = spread * jax.random.normal(key, shape, jnp.float32)
    if pieces:
        entries = entries * level_of(key, shape, pieces, -0.22, 0.18)
    return jnp.clip(entries, -limit, limit).astype(held_as)


def setup_inputs(seed: int = 0) -> dict:
    keys = jax.random.split(jax.random.key(seed), 7)
    return {
        "frames": centred(keys[0], (FRAMES, MODULES * PIX), 1.0, 6.0, ((0, 8), (1, 16))),
        "weights": jnp.clip(0.25 * jax.random.uniform(keys[1], (MODULES * TPM, PB, TILE), jnp.float32) ** level_of(keys[1], (MODULES * TPM, PB, TILE), ((0, 16),), -0.2, 0.2), 0.0, 0.25).astype(jnp.bfloat16),
        "monitor": jnp.clip(jnp.exp(math.log(2.0) - 1.3862944 * jax.random.uniform(keys[2], (FRAMES,), jnp.float32) ** level_of(keys[2], (FRAMES,), ((0, 8),), -0.2, 0.2)), 0.5, 2.0),
        "coverage": draw_coverage(jax.random.fold_in(keys[6], 71), 0),
        "block_slot": jax.vmap(lambda own: jax.random.permutation(own, TPM))(jax.random.split(keys[4], MODULES)).reshape((MODULES, TPM)).astype(jnp.int32),
        "angle_index": place_ends(jax.random.randint(keys[5], (ANGLES,), 0, ASTEPS), jax.random.fold_in(keys[5], 1), 0, ASTEPS - 1).astype(jnp.int32),
    }


def ramp_table(length):
    places = jnp.arange(length, dtype=jnp.int32)
    offset = places[:, None] - places[None, :]
    is_odd = (offset % 2) != 0
    scaled = math.pi * offset.astype(jnp.float32)
    safe_den = jnp.where(is_odd, scaled, jnp.float32(1.0))
    return jnp.where(offset == 0, jnp.float32(0.25), jnp.where(is_odd, -1.0 / (safe_den * safe_den), jnp.float32(0.0)))


def spot_table(angle_index, row_count, length):
    theta_rad = angle_index.astype(jnp.float32) * (math.pi / ASTEPS)
    centre = (length - 1) / 2.0
    across = jnp.arange(length, dtype=jnp.float32) - centre
    down_pos = jnp.arange(row_count, dtype=jnp.float32) - (row_count - 1) / 2.0
    spot_grid = across[None, None, :] * jnp.cos(theta_rad)[:, None, None] + down_pos[None, :, None] * jnp.sin(theta_rad)[:, None, None] + centre
    return spot_grid.reshape(angle_index.shape[0], row_count * length)


def rounded_weight(spot_grid, node_pos):
    weight_val = jnp.maximum(0.0, 1.0 - jnp.abs(spot_grid - node_pos)).astype(jnp.bfloat16)
    weight_val = lax.optimization_barrier(weight_val)
    return weight_val.astype(jnp.float32)


def reference(frames, weights, monitor, coverage, block_slot, angle_index):
    group_count = TPM // SPLITS
    pixel_count = group_count * PB

    def add_module(summed, module_pos):
        module_frames = lax.dynamic_slice_in_dim(frames, module_pos * pixel_count, pixel_count, 1)
        module_frames = module_frames.astype(jnp.float32).reshape(FRAMES, group_count, PB)
        module_tiles = lax.dynamic_slice_in_dim(weights, module_pos * TPM, TPM, 0)
        module_tiles = module_tiles.astype(jnp.float32).reshape(group_count, SPLITS, PB, TILE)
        block_bins = jnp.einsum("fgp,gspc->fgsc", module_frames, module_tiles).reshape(FRAMES, TPM, TILE)
        tile_ids = coverage[module_pos][block_slot[module_pos]]
        return summed.at[:, tile_ids, :].add(block_bins), None

    summed, _ = lax.scan(add_module, jnp.zeros((FRAMES, NTILE, TILE), jnp.float32), jnp.arange(MODULES, dtype=jnp.int32))
    binned = (summed / monitor[:, None, None]).reshape(ANGLES, TRANS, NTILE * TILE)
    filtered = jnp.einsum("apb,pq->abq", binned, ramp_table(TRANS), precision=lax.Precision.HIGHEST).astype(jnp.bfloat16)

    spot_grid = spot_table(angle_index, ROWS, TRANS)
    lower_pos = jnp.floor(spot_grid)
    upper_pos = lower_pos + 1.0
    w_lower = rounded_weight(spot_grid, lower_pos)
    w_upper = rounded_weight(spot_grid, upper_pos)
    w_lower = jnp.where((lower_pos >= 0.0) & (lower_pos <= TRANS - 1.0), w_lower, 0.0)
    w_upper = jnp.where((upper_pos >= 0.0) & (upper_pos <= TRANS - 1.0), w_upper, 0.0)
    idx_lower = jnp.clip(lower_pos, 0.0, TRANS - 1.0).astype(jnp.int32)
    idx_upper = jnp.clip(upper_pos, 0.0, TRANS - 1.0).astype(jnp.int32)

    tile_major = filtered.reshape(ANGLES, NTILE, TILE, TRANS).transpose(1, 0, 2, 3)

    def one_tile(values):
        values = values.astype(jnp.float32)
        low_pick = jnp.take_along_axis(values, jnp.broadcast_to(idx_lower[:, None, :], (ANGLES, TILE, ROWS * TRANS)), axis=2)
        high_pick = jnp.take_along_axis(values, jnp.broadcast_to(idx_upper[:, None, :], (ANGLES, TILE, ROWS * TRANS)), axis=2)
        return jnp.sum(low_pick * w_lower[:, None, :] + high_pick * w_upper[:, None, :], axis=0)

    slices = lax.map(one_tile, tile_major)
    slices = (slices * (math.pi / ANGLES)).astype(jnp.bfloat16)
    return slices.reshape(QT, GROUPS, MODULES, TILE, ROWS * TRANS)
```

```python
import functools
import math

import jax
import jax.numpy as jnp
from jax import lax
from jax.experimental import pallas as pl
from jax.experimental.pallas import tpu as pltpu
from jax.sharding import PartitionSpec as P

TRANS = 512
ASTEPS = 180
ROWS = 16
NTILE = 256
SIDE = 4
CHUNKS = (128, 128)
RELAY = (False, False)
FAR = (1, 3, 2)
WINDOW = 256

VMEM = pltpu.MemorySpace.VMEM
MIB = 1 << 20


def ramp_table(length):
    places = jnp.arange(length, dtype=jnp.int32)
    offset = places[:, None] - places[None, :]
    is_odd = offset % 2 != 0
    scaled = math.pi * offset.astype(jnp.float32)
    safe_den = jnp.where(is_odd, scaled, jnp.float32(1.0))
    return jnp.where(
        offset == 0,
        jnp.float32(0.25),
        jnp.where(is_odd, -1.0 / (safe_den * safe_den), jnp.float32(0.0)),
    )


def spot_table(angle_index, row_count, length):
    theta_rad = angle_index.astype(jnp.float32) * (math.pi / ASTEPS)
    centre = (length - 1) / 2.0
    across = jnp.arange(length, dtype=jnp.float32) - centre
    down_pos = jnp.arange(row_count, dtype=jnp.float32) - (row_count - 1) / 2.0
    return (
        across[None, None, :] * jnp.cos(theta_rad)[:, None, None]
        + down_pos[None, :, None] * jnp.sin(theta_rad)[:, None, None]
        + centre
    )


def bin_kernel(slot_ref, cover_ref, mon_ref, fr_ref, wt_ref, *rest, begin):
    outs, (pixels, tiles, hold, sem, out_sem) = rest[:-5], rest[-5:]
    groups = sem.shape[1]
    depth = pixels.shape[1] // groups
    splits = tiles.shape[0] // groups
    width = tiles.shape[2]
    rows, half = pixels.shape[0], hold.shape[2]
    span = hold.shape[1] // (SIDE * SIDE)

    def fetch(g):
        across = pl.ds(pl.multiple_of(g * depth, depth), depth)
        return (
            pltpu.make_async_copy(
                wt_ref.at[pl.ds(g * splits, splits)],
                tiles.at[pl.ds(g * splits, splits)],
                sem.at[0, g],
            ),
            pltpu.make_async_copy(
                fr_ref.at[pl.ds(begin, rows), across], pixels.at[:, across], sem.at[1, g]
            ),
        )

    for g in range(groups):
        for copy in fetch(g):
            copy.start()
    me = lax.axis_index("module")
    z, x = me // SIDE, me % SIDE
    first = cover_ref[me, 0]
    scale = 1.0 / mon_ref[...]

    def one(g, carry):
        for copy in fetch(g):
            copy.wait()
        across = pl.ds(pl.multiple_of(g * depth, depth), depth)
        here = jnp.concatenate([tiles[g * splits + s] for s in range(splits)], axis=1)
        bins = jnp.dot(pixels[:, across], here, preferred_element_type=jnp.float32)
        bins = bins * scale
        for s in range(splits):
            slot = slot_ref[0, g * splits + s]
            owner = (first + slot) & (SIDE * SIDE - 1)
            turn = slot // (SIDE * SIDE)
            away_z = (owner // SIDE - z) & (SIDE - 1)
            away_x = (owner - x) & (SIDE - 1)
            cut = slice(s * width, (s + 1) * width)
            hold[0, (away_x * SIDE + away_z) * span + turn] = bins[:half, cut]
            hold[1, (away_z * SIDE + away_x) * span + turn] = bins[half:, cut]
        return carry

    lax.fori_loop(0, groups, one, 0)
    each = outs[0].shape[0]
    copies = [
        pltpu.make_async_copy(
            hold.at[n // SIDE, pl.ds(n % SIDE * each, each)], out, out_sem.at[n]
        )
        for n, out in enumerate(outs)
    ]
    for copy in copies:
        copy.start()
    for copy in copies:
        copy.wait()


def bin_chunk(block_slot, coverage, frames, weights, monitor, begin, rows):
    pixels = frames.shape[1]
    slots, group_pixels, width = weights.shape
    groups = pixels // group_pixels
    half = rows // 2
    each = slots // SIDE
    smem = pl.BlockSpec(memory_space=pltpu.MemorySpace.SMEM)
    anywhere = pl.BlockSpec(memory_space=pl.ANY)
    in_hbm = pl.BlockSpec(memory_space=pltpu.MemorySpace.HBM)
    return pl.pallas_call(
        functools.partial(bin_kernel, begin=begin),
        out_shape=[jax.ShapeDtypeStruct((each, half, width), jnp.float32)] * (2 * SIDE),
        in_specs=[smem, smem, pl.BlockSpec(memory_space=VMEM), in_hbm, in_hbm],
        out_specs=[anywhere] * (2 * SIDE),
        scratch_shapes=[
            pltpu.VMEM((rows, pixels), frames.dtype),
            pltpu.VMEM(weights.shape, weights.dtype),
            pltpu.VMEM((2, slots, half, width), jnp.float32),
            pltpu.SemaphoreType.DMA((2, groups)),
            pltpu.SemaphoreType.DMA((2 * SIDE,)),
        ],
        compiler_params=pltpu.CompilerParams(vmem_limit_bytes=(26 if begin else 55) * MIB),
        cost_estimate=pl.CostEstimate(
            flops=2 * rows * pixels * slots // groups * width,
            bytes_accessed=2 * slots * group_pixels * width + 6 * rows * pixels,
            transcendentals=0,
        ),
    )(block_slot, coverage, monitor[begin : begin + rows, None], frames, weights)


def merge_kernel(cover_ref, *rest, axis, relay):
    sources, outs = rest[:SIDE], rest[SIDE:]
    span = sources[0].shape[0] // SIDE
    modules = SIDE * SIDE
    tiles = NTILE // modules
    half = tiles // 2
    me = lax.axis_index("module")
    z, x = me // SIDE, me % SIDE
    if relay:
        keep0, keep1, keep3, plus, minus = outs
        parts = [
            (2, 0, plus.at[0]),
            (2, 1, minus.at[0]),
            (1, 0, keep1),
            (1, 1, plus.at[1]),
            (3, 0, minus.at[1]),
            (3, 1, keep3),
            (0, 0, keep0.at[pl.ds(0, half)]),
            (0, 1, keep0.at[pl.ds(half, half)]),
        ]
    else:
        parts = [(e, p, outs[e].at[pl.ds(p * half, half)]) for e in range(SIDE) for p in range(2)]
    for e, part, out in parts:
        begin = []
        for d in range(SIDE):
            if axis == "x":
                source = z * SIDE + ((x - d) & (SIDE - 1))
                owner = ((z + e) & (SIDE - 1)) * SIDE + x
            else:
                source = ((z - d) & (SIDE - 1)) * SIDE + x
                owner = z * SIDE + ((x + e) & (SIDE - 1))
            first = cover_ref[source, 0]
            skip = (owner - first) & (modules - 1)
            begin.append(((first + skip) // modules) & (tiles - 1))

        def one(k, carry, e=e, part=part, begin=begin, out=out):
            total = None
            for d in range(SIDE):
                j = (k + part * half - begin[d]) & (tiles - 1)
                tile = sources[d][e * span + jnp.minimum(j, span - 1)]
                tile = jnp.where(j < span, tile, 0.0)
                total = tile if total is None else total + tile
            out[k] = total
            return carry

        lax.fori_loop(0, half, one, 0)


def merge(coverage, sources, axis, relay):
    each, rows, width = sources[0].shape
    tiles = NTILE // (SIDE * SIDE)
    half = tiles // 2

    def shape(*lead):
        return jax.ShapeDtypeStruct((*lead, rows, width), jnp.float32)

    if relay:
        outs = [shape(tiles), shape(half), shape(half), shape(2, half), shape(2, half)]
    else:
        outs = [shape(tiles)] * SIDE
    return pl.pallas_call(
        functools.partial(merge_kernel, axis=axis, relay=relay),
        out_shape=outs,
        in_specs=[pl.BlockSpec(memory_space=pltpu.MemorySpace.SMEM)]
        + [pl.BlockSpec(memory_space=VMEM)] * SIDE,
        out_specs=[pl.BlockSpec(memory_space=VMEM)] * len(outs),
        compiler_params=pltpu.CompilerParams(vmem_limit_bytes=14 * MIB),
        cost_estimate=pl.CostEstimate(
            flops=4 * 64 * rows * width,
            bytes_accessed=4 * rows * width * (4 * each + 64),
            transcendentals=0,
        ),
    )(coverage, *sources)


def join_kernel(*refs, relay):
    count = 5 if relay else 4
    outs = refs[2 * count :]
    me = lax.axis_index("frame")
    y, core = me // 2, me % 2
    half = refs[0].shape[0] // 2
    for n, out in enumerate(outs):
        owner = ((y + n // 2) & (SIDE - 1)) * 2 + (core ^ (n % 2))
        for side in range(2):
            parts = refs[count * side : count * (side + 1)]
            if relay:
                keep0, plus, minus, far_plus, far_minus = parts
                out[side] = keep0[owner] + minus[1, owner] + far_plus[owner]
                out[2 + side] = keep0[half + owner] + plus[1, owner] + far_minus[owner]
            else:
                for q in range(2):
                    k = q * half + owner
                    out[2 * q + side] = parts[0][k] + parts[1][k] + (parts[2][k] + parts[3][k])


def join(parts, relay):
    tiles, rows, width = parts[0].shape
    half = tiles // 2
    return pl.pallas_call(
        functools.partial(join_kernel, relay=relay),
        out_shape=[jax.ShapeDtypeStruct((4, rows, width), jnp.float32)] * half,
        in_specs=[pl.BlockSpec(memory_space=VMEM)] * len(parts),
        out_specs=[pl.BlockSpec(memory_space=VMEM)] * half,
        compiler_params=pltpu.CompilerParams(vmem_limit_bytes=14 * MIB),
        cost_estimate=pl.CostEstimate(
            flops=8 * half * rows * width,
            bytes_accessed=4 * rows * width * half * 18,
            transcendentals=0,
        ),
    )(*parts)


def split(value):
    high = value.astype(jnp.bfloat16)
    return high, (value - high.astype(jnp.float32)).astype(jnp.bfloat16)


def filter_kernel(ramp_ref, *rest, begin, count):
    lines, out = rest[:count], rest[-1]
    prev = rest[count] if len(rest) == count + 2 else None
    rows = 2 * lines[0].shape[1]
    width = lines[0].shape[2]
    me = lax.axis_index("frame")
    y, core = me // 2, me % 2
    per_group = ramp_ref.shape[0] // 2
    ramp = jnp.concatenate(
        [ramp_ref[pl.ds((core ^ dc) * per_group + begin, rows), :] for dc in range(2)], axis=0
    )
    ramp_high, ramp_low = split(ramp)
    for dy in range(SIDE):
        a = (y - dy) & (SIDE - 1)
        for q in range(2):
            both = [
                lines[2 * dy + dc][2 * q : 2 * q + 2].reshape(rows, width) for dc in range(2)
            ]
            high, low = split(jnp.concatenate(both, axis=0).T)
            total = jnp.dot(high, ramp_high, preferred_element_type=jnp.float32)
            total = total + jnp.dot(high, ramp_low, preferred_element_type=jnp.float32)
            total = total + jnp.dot(low, ramp_high, preferred_element_type=jnp.float32)
            here = slice(q * width, (q + 1) * width)
            if prev is not None:
                total = total + prev[a, here]
            out[a, here] = total.astype(out.dtype)


def ramp_chunk(ramp, lines, prev, begin, last, angles):
    width = lines[0].shape[2]
    length = ramp.shape[0]
    operands = [ramp, *lines] + ([] if prev is None else [prev])
    return pl.pallas_call(
        functools.partial(filter_kernel, begin=begin, count=len(lines)),
        out_shape=jax.ShapeDtypeStruct(
            (angles, 2 * width, length), jnp.bfloat16 if last else jnp.float32
        ),
        in_specs=[pl.BlockSpec(memory_space=VMEM)] * len(operands),
        out_specs=pl.BlockSpec(memory_space=VMEM),
        compiler_params=pltpu.CompilerParams(vmem_limit_bytes=14 * MIB),
        cost_estimate=pl.CostEstimate(
            flops=6 * angles * 2 * width * length * length // 2,
            bytes_accessed=4 * len(lines) * lines[0].size + 8 * angles * width * length,
            transcendentals=0,
        ),
    )(*operands)


def table_kernel(start_ref, spot_ref, out_ref):
    pair = pl.program_id(0)
    strips, angles, window, cols = out_ref.shape[1:]
    rank = lax.broadcasted_iota(jnp.int32, (window, cols), 0)
    for strip in range(strips):
        for a in range(angles):
            n = strip * angles + a
            place = (rank + start_ref[pair, n] * 128).astype(jnp.float32)
            spot = spot_ref[0, n : n + 1, :]
            out_ref[0, strip, a] = jnp.maximum(0.0, 1.0 - jnp.abs(spot - place)).astype(
                jnp.bfloat16
            )


def make_tables(start, spots, angles):
    pairs, count, cols = spots.shape
    strips = count // angles
    return pl.pallas_call(
        table_kernel,
        name="tables",
        out_shape=jax.ShapeDtypeStruct((pairs, strips, angles, WINDOW, cols), jnp.bfloat16),
        grid_spec=pltpu.PrefetchScalarGridSpec(
            num_scalar_prefetch=1,
            grid=(pairs,),
            in_specs=[pl.BlockSpec((1, count, cols), lambda i, start: (i, 0, 0))],
            out_specs=pl.BlockSpec(
                (1, strips, angles, WINDOW, cols), lambda i, start: (i, 0, 0, 0, 0)
            ),
        ),
        compiler_params=pltpu.CompilerParams(vmem_limit_bytes=10 * MIB),
        cost_estimate=pl.CostEstimate(
            flops=5 * pairs * count * WINDOW * cols,
            bytes_accessed=2 * pairs * count * WINDOW * cols,
            transcendentals=0,
        ),
    )(start, spots)


def back_kernel(start_ref, filt_ref, tables, out_ref, done, out_sem, *, scale):
    pairs, strips, angles, _, cols = tables.shape
    cols = cols // 2
    line = done.shape[1] // (2 * pairs)

    def put(pair):
        across = pl.ds(pl.multiple_of(pair * 2 * line, 2 * line), 2 * line)
        return pltpu.make_async_copy(done.at[:, across], out_ref.at[:, across], out_sem.at[pair])

    def one(pair, carry):
        for strip in range(strips):
            total = None
            for a in range(angles):
                begin = pl.multiple_of(start_ref[pair, strip * angles + a] * 128, 128)
                part = jnp.dot(
                    filt_ref[a, :, pl.ds(begin, WINDOW)],
                    tables[pair, strip, a],
                    preferred_element_type=jnp.float32,
                )
                total = part if total is None else total + part
            total = (total * scale).astype(jnp.bfloat16)
            for r in range(2):
                to = pl.multiple_of(pair * 2 * line + r * line + strip * cols, 128)
                done[:, pl.ds(to, cols)] = total[:, r * cols : (r + 1) * cols]
        put(pair).start()
        return carry

    lax.fori_loop(0, pairs, one, 0)
    for pair in range(pairs):
        put(pair).wait()


def back_project(start, filt, tables):
    angles, bins, length = filt.shape
    pairs, strips, _, window, cols = tables.shape
    columns = pairs * 2 * length
    return pl.pallas_call(
        functools.partial(back_kernel, scale=math.pi / angles),
        name="back",
        out_shape=jax.ShapeDtypeStruct((bins, columns), jnp.bfloat16),
        in_specs=[
            pl.BlockSpec(memory_space=pltpu.MemorySpace.SMEM),
            pl.BlockSpec(memory_space=VMEM),
            pl.BlockSpec(memory_space=VMEM),
        ],
        out_specs=pl.BlockSpec(memory_space=pl.ANY),
        scratch_shapes=[
            pltpu.VMEM((bins, columns), jnp.bfloat16),
            pltpu.SemaphoreType.DMA((pairs,)),
        ],
        compiler_params=pltpu.CompilerParams(vmem_limit_bytes=24 * MIB),
        cost_estimate=pl.CostEstimate(
            flops=2 * bins * pairs * strips * angles * window * cols,
            bytes_accessed=2 * tables.size + 2 * bins * columns,
            transcendentals=0,
        ),
    )(start, filt, tables)


def shift(array, axis, by):
    pairs = []
    for z in range(SIDE):
        for x in range(SIDE):
            to = (z, (x + by) % SIDE) if axis == "x" else ((z + by) % SIDE, x)
            pairs.append((z * SIDE + x, to[0] * SIDE + to[1]))
    return lax.ppermute(array, "module", pairs)


def swap(array, by, cross):
    pairs = []
    for y in range(SIDE):
        for core in range(2):
            pairs.append((y * 2 + core, (y + by) % SIDE * 2 + (core ^ cross)))
    return lax.ppermute(array, "frame", pairs)


def on_device(frames, weights, monitor, coverage, block_slot, angle_index):
    angles = angle_index.shape[0]
    spots = spot_table(angle_index, ROWS, TRANS)
    spots = spots.reshape(angles, ROWS // 2, 2, TRANS // 128, 128)
    spots = spots.transpose(1, 3, 0, 2, 4).reshape(ROWS // 2, TRANS // 128 * angles, 256)
    start = jnp.floor(jnp.min(spots, axis=2) / 128.0).astype(jnp.int32)
    start = jnp.clip(start, 0, (TRANS - WINDOW) // 128)

    def first_leg(sent):
        halves = [[sent[0]], [sent[SIDE]]]
        for d in FAR:
            for side, axis in enumerate("xz"):
                halves[side].append((d, shift(sent[side * SIDE + d], axis, d)))
        return [[own] + [a for _, a in sorted(rest, key=lambda p: p[0])] for own, *rest in halves]

    def second_leg(halves, relay):
        parts = []
        kept = []
        for side, (axis, other) in enumerate((("x", "z"), ("z", "x"))):
            outs = merge(coverage, halves[side], axis, relay)
            if relay:
                keep0, keep1, keep3, plus, minus = outs
                kept.append((keep0, keep1, keep3, shift(plus, other, 1), shift(minus, other, -1)))
            else:
                parts += [outs[0]] + [shift(outs[e], other, e) for e in (1, 2, 3)]
        for side, other in enumerate("zx"):
            if relay:
                keep0, keep1, keep3, plus, minus = kept[side]
                far_plus = shift(keep1 + plus[0], other, 1)
                far_minus = shift(keep3 + minus[0], other, -1)
                parts += [keep0, plus, minus, far_plus, far_minus]
        own, *others = join(parts, relay)
        return [own] + [swap(o, n // 2, n % 2) for n, o in enumerate(others, 1)]

    begins = [sum(CHUNKS[:c]) for c in range(len(CHUNKS))]
    sent = [
        bin_chunk(block_slot, coverage, frames, weights, monitor, begin, rows)
        for begin, rows in zip(begins, CHUNKS)
    ]
    filt = None
    arrived = first_leg(sent[0])
    ramp = ramp_table(TRANS)
    tables = make_tables(start, spots, angles)
    for c, begin in enumerate(begins):
        here = arrived
        last = c + 1 == len(CHUNKS)
        if not last:
            extra = (ramp, tables) if c == 0 else ()
            held = []
            for side in range(2):
                ready = sent[c + 1][side * SIDE : (side + 1) * SIDE]
                ready, here[side], extra = lax.optimization_barrier((ready, here[side], extra))
                held += ready
            if c == 0:
                ramp, tables = extra
            arrived = first_leg(held)
        lines = second_leg(here, RELAY[c])
        filt = ramp_chunk(ramp, lines, filt, begin, last, angles)
    slices = back_project(start, filt, tables)
    return slices.reshape(2, 1, 1, slices.shape[0] // 2, slices.shape[1])


def solution(mesh):
    placed = (
        P("frame", "module"),
        P("module", None, None),
        P("frame"),
        P(),
        P("module", None),
        P(),
    )
    return jax.shard_map(
        on_device,
        mesh=mesh,
        in_specs=placed,
        out_specs=P(None, "frame", "module", None, None),
        check_vma=False,
    )
```

```python
import functools
import math

import jax
import jax.numpy as jnp
from jax import lax
from jax.experimental import pallas as pl
from jax.experimental.pallas import tpu as pltpu
from jax.sharding import PartitionSpec as P

TRANS = 512
ASTEPS = 180
ROWS = 16
NTILE = 256
SIDE = 4
CHUNKS = (128, 128)
RELAY = (False, False)
FAR = (2, 1, 3)
UNROLL = 4
AHEAD = 8
WINDOW = 256

VMEM = pltpu.MemorySpace.VMEM
MIB = 1 << 20
FIRST_MIB = 52


def ramp_table(length):
    places = jnp.arange(length, dtype=jnp.int32)
    offset = places[:, None] - places[None, :]
    is_odd = offset % 2 != 0
    scaled = math.pi * offset.astype(jnp.float32)
    safe_den = jnp.where(is_odd, scaled, jnp.float32(1.0))
    return jnp.where(
        offset == 0,
        jnp.float32(0.25),
        jnp.where(is_odd, -1.0 / (safe_den * safe_den), jnp.float32(0.0)),
    )


def spot_table(angle_index, row_count, length):
    theta_rad = angle_index.astype(jnp.float32) * (math.pi / ASTEPS)
    centre = (length - 1) / 2.0
    across = jnp.arange(length, dtype=jnp.float32) - centre
    down_pos = jnp.arange(row_count, dtype=jnp.float32) - (row_count - 1) / 2.0
    return (
        across[None, None, :] * jnp.cos(theta_rad)[:, None, None]
        + down_pos[None, :, None] * jnp.sin(theta_rad)[:, None, None]
        + centre
    )


def bin_kernel(slot_any, cover_any, mon_any, fr_ref, wt_ref, *rest, begin):
    outs = rest[:-9]
    pixels, tiles, hold, slot_ref, cover_ref, mon_ref, sem, out_sem, small_sem = rest[-9:]
    small = [
        pltpu.make_async_copy(mon_any, mon_ref, small_sem.at[2]),
        pltpu.make_async_copy(slot_any, slot_ref, small_sem.at[0]),
        pltpu.make_async_copy(cover_any, cover_ref, small_sem.at[1]),
    ]
    for copy in small:
        copy.start()
    groups = sem.shape[1]
    depth = pixels.shape[1] // groups
    splits = tiles.shape[0] // groups
    width = tiles.shape[2]
    rows, half = pixels.shape[0], hold.shape[2]
    span = hold.shape[1] // (SIDE * SIDE)

    def fetch(g):
        across = pl.ds(pl.multiple_of(g * depth, depth), depth)
        return (
            pltpu.make_async_copy(
                wt_ref.at[pl.ds(g * splits, splits)],
                tiles.at[pl.ds(g * splits, splits)],
                sem.at[0, g],
            ),
            pltpu.make_async_copy(
                fr_ref.at[pl.ds(begin, rows), across], pixels.at[:, across], sem.at[1, g]
            ),
        )

    for g in range(AHEAD):
        for copy in fetch(g):
            copy.start()
    me = lax.axis_index("module")
    z, x = me // SIDE, me % SIDE
    for copy in small:
        copy.wait()
    flux = mon_ref[0:1, pl.ds(begin, rows)]
    diagonal = lax.broadcasted_iota(jnp.int32, (rows, rows), 0) == lax.broadcasted_iota(
        jnp.int32, (rows, rows), 1
    )
    scale = 1.0 / jnp.sum(jnp.where(diagonal, flux, 0.0), axis=1, keepdims=True)
    first = cover_ref[me, 0]

    def one(turn_pos, carry):
        base = turn_pos * UNROLL
        for u in range(UNROLL):
            for copy in fetch(base + u):
                copy.wait()

        @pl.when(base + AHEAD < groups)
        def _():
            for u in range(UNROLL):
                for copy in fetch(base + AHEAD + u):
                    copy.start()

        for u in range(UNROLL):
            g = base + u
            across = pl.ds(pl.multiple_of(g * depth, depth), depth)
            here = jnp.concatenate([tiles[g * splits + s] for s in range(splits)], axis=1)
            bins = jnp.dot(pixels[:, across], here, preferred_element_type=jnp.float32)
            bins = bins * scale
            for s in range(splits):
                slot = slot_ref[0, g * splits + s]
                owner = (first + slot) & (SIDE * SIDE - 1)
                turn = slot // (SIDE * SIDE)
                away_z = (owner // SIDE - z) & (SIDE - 1)
                away_x = (owner - x) & (SIDE - 1)
                cut = slice(s * width, (s + 1) * width)
                hold[0, (away_x * SIDE + away_z) * span + turn] = bins[:half, cut]
                hold[1, (away_z * SIDE + away_x) * span + turn] = bins[half:, cut]
        return carry

    lax.fori_loop(0, groups // UNROLL, one, 0)
    each = outs[0].shape[0]
    copies = [
        pltpu.make_async_copy(
            hold.at[n // SIDE, pl.ds(n % SIDE * each, each)], out, out_sem.at[n]
        )
        for n, out in enumerate(outs)
    ]
    for copy in copies:
        copy.start()
    for copy in copies:
        copy.wait()


def stay(value):
    return pltpu.with_memory_space_constraint(value, pltpu.MemorySpace.HBM)


def bin_chunk(block_slot, coverage, frames, weights, monitor, begin, rows, tag):
    pixels = frames.shape[1]
    slots, group_pixels, width = weights.shape
    groups = pixels // group_pixels
    half = rows // 2
    each = slots // SIDE
    anywhere = pl.BlockSpec(memory_space=pl.ANY)
    in_hbm = pl.BlockSpec(memory_space=pltpu.MemorySpace.HBM)
    return pl.pallas_call(
        functools.partial(bin_kernel, begin=begin),
        out_shape=[jax.ShapeDtypeStruct((each, half, width), jnp.float32)] * (2 * SIDE),
        in_specs=[in_hbm] * 5,
        out_specs=[in_hbm if n % SIDE == 0 else anywhere for n in range(2 * SIDE)],
        scratch_shapes=[
            pltpu.VMEM((rows, pixels), frames.dtype),
            pltpu.VMEM(weights.shape, weights.dtype),
            pltpu.VMEM((2, slots, half, width), jnp.float32),
            pltpu.SMEM(block_slot.shape, jnp.int32),
            pltpu.SMEM(coverage.shape, jnp.int32),
            pltpu.VMEM((1, monitor.size), monitor.dtype),
            pltpu.SemaphoreType.DMA((2, groups)),
            pltpu.SemaphoreType.DMA((2 * SIDE,)),
            pltpu.SemaphoreType.DMA((3,)),
        ],
        compiler_params=pltpu.CompilerParams(vmem_limit_bytes=(26 if tag else FIRST_MIB) * MIB),
        cost_estimate=pl.CostEstimate(
            flops=2 * rows * pixels * slots // groups * width,
            bytes_accessed=2 * slots * group_pixels * width + 6 * rows * pixels,
            transcendentals=0,
        ),
    )(*(stay(v) for v in (block_slot, coverage, monitor.reshape(1, -1), frames, weights)))


def merge_kernel(cover_ref, *rest, axis, relay):
    sources, outs = rest[:SIDE], rest[SIDE:]
    span = sources[0].shape[0] // SIDE
    modules = SIDE * SIDE
    tiles = NTILE // modules
    half = tiles // 2
    me = lax.axis_index("module")
    z, x = me // SIDE, me % SIDE
    if relay:
        keep0, keep1, keep3, plus, minus = outs
        parts = [
            (2, 0, plus.at[0]),
            (2, 1, minus.at[0]),
            (1, 0, keep1),
            (1, 1, plus.at[1]),
            (3, 0, minus.at[1]),
            (3, 1, keep3),
            (0, 0, keep0.at[pl.ds(0, half)]),
            (0, 1, keep0.at[pl.ds(half, half)]),
        ]
    else:
        parts = [(e, p, outs[e].at[pl.ds(p * half, half)]) for e in range(SIDE) for p in range(2)]
    for e, part, out in parts:
        begin = []
        for d in range(SIDE):
            if axis == "x":
                source = z * SIDE + ((x - d) & (SIDE - 1))
                owner = ((z + e) & (SIDE - 1)) * SIDE + x
            else:
                source = ((z - d) & (SIDE - 1)) * SIDE + x
                owner = z * SIDE + ((x + e) & (SIDE - 1))
            first = cover_ref[source, 0]
            skip = (owner - first) & (modules - 1)
            begin.append(((first + skip) // modules) & (tiles - 1))

        def one(k, carry, e=e, part=part, begin=begin, out=out):
            total = None
            for d in range(SIDE):
                j = (k + part * half - begin[d]) & (tiles - 1)
                tile = sources[d][e * span + jnp.minimum(j, span - 1)]
                tile = jnp.where(j < span, tile, 0.0)
                total = tile if total is None else total + tile
            out[k] = total
            return carry

        lax.fori_loop(0, half, one, 0)


def merge(coverage, sources, axis, relay):
    each, rows, width = sources[0].shape
    tiles = NTILE // (SIDE * SIDE)
    half = tiles // 2

    def shape(*lead):
        return jax.ShapeDtypeStruct((*lead, rows, width), jnp.float32)

    if relay:
        outs = [shape(tiles), shape(half), shape(half), shape(2, half), shape(2, half)]
    else:
        outs = [shape(tiles)] * SIDE
    return pl.pallas_call(
        functools.partial(merge_kernel, axis=axis, relay=relay),
        out_shape=outs,
        in_specs=[pl.BlockSpec(memory_space=pltpu.MemorySpace.SMEM)]
        + [pl.BlockSpec(memory_space=VMEM)] * SIDE,
        out_specs=[pl.BlockSpec(memory_space=VMEM)] * len(outs),
        compiler_params=pltpu.CompilerParams(vmem_limit_bytes=14 * MIB),
        cost_estimate=pl.CostEstimate(
            flops=4 * 64 * rows * width,
            bytes_accessed=4 * rows * width * (4 * each + 64),
            transcendentals=0,
        ),
    )(coverage, *sources)


def join_kernel(*refs, relay):
    count = 5 if relay else 4
    outs = refs[2 * count :]
    me = lax.axis_index("frame")
    y, core = me // 2, me % 2
    half = refs[0].shape[0] // 2
    for n, out in enumerate(outs):
        owner = ((y + n // 2) & (SIDE - 1)) * 2 + (core ^ (n % 2))
        for side in range(2):
            parts = refs[count * side : count * (side + 1)]
            if relay:
                keep0, plus, minus, far_plus, far_minus = parts
                out[side] = keep0[owner] + minus[1, owner] + far_plus[owner]
                out[2 + side] = keep0[half + owner] + plus[1, owner] + far_minus[owner]
            else:
                for q in range(2):
                    k = q * half + owner
                    out[2 * q + side] = parts[0][k] + parts[1][k] + (parts[2][k] + parts[3][k])


def join(parts, relay):
    tiles, rows, width = parts[0].shape
    half = tiles // 2
    return pl.pallas_call(
        functools.partial(join_kernel, relay=relay),
        out_shape=[jax.ShapeDtypeStruct((4, rows, width), jnp.float32)] * half,
        in_specs=[pl.BlockSpec(memory_space=VMEM)] * len(parts),
        out_specs=[pl.BlockSpec(memory_space=VMEM)] * half,
        compiler_params=pltpu.CompilerParams(vmem_limit_bytes=14 * MIB),
        cost_estimate=pl.CostEstimate(
            flops=8 * half * rows * width,
            bytes_accessed=4 * rows * width * half * 18,
            transcendentals=0,
        ),
    )(*parts)


def split(value):
    high = value.astype(jnp.bfloat16)
    return high, (value - high.astype(jnp.float32)).astype(jnp.bfloat16)


def filter_kernel(ramp_ref, *rest, begin, count):
    lines, out = rest[:count], rest[-1]
    prev = rest[count] if len(rest) == count + 2 else None
    rows = 2 * lines[0].shape[1]
    width = lines[0].shape[2]
    me = lax.axis_index("frame")
    y, core = me // 2, me % 2
    per_group = ramp_ref.shape[0] // 2
    ramp = jnp.concatenate(
        [ramp_ref[pl.ds((core ^ dc) * per_group + begin, rows), :] for dc in range(2)], axis=0
    )
    ramp_high, ramp_low = split(ramp)
    for dy in range(SIDE):
        a = (y - dy) & (SIDE - 1)
        for q in range(2):
            both = [
                lines[2 * dy + dc][2 * q : 2 * q + 2].reshape(rows, width) for dc in range(2)
            ]
            high, low = split(jnp.concatenate(both, axis=0).T)
            total = jnp.dot(high, ramp_high, preferred_element_type=jnp.float32)
            total = total + jnp.dot(high, ramp_low, preferred_element_type=jnp.float32)
            total = total + jnp.dot(low, ramp_high, preferred_element_type=jnp.float32)
            here = slice(q * width, (q + 1) * width)
            if prev is not None:
                total = total + prev[a, here]
            out[a, here] = total.astype(out.dtype)


def ramp_chunk(ramp, lines, prev, begin, last, angles):
    width = lines[0].shape[2]
    length = ramp.shape[0]
    operands = [ramp, *lines] + ([] if prev is None else [prev])
    return pl.pallas_call(
        functools.partial(filter_kernel, begin=begin, count=len(lines)),
        out_shape=jax.ShapeDtypeStruct(
            (angles, 2 * width, length), jnp.bfloat16 if last else jnp.float32
        ),
        in_specs=[pl.BlockSpec(memory_space=VMEM)] * len(operands),
        out_specs=pl.BlockSpec(memory_space=VMEM),
        compiler_params=pltpu.CompilerParams(vmem_limit_bytes=14 * MIB),
        cost_estimate=pl.CostEstimate(
            flops=6 * angles * 2 * width * length * length // 2,
            bytes_accessed=4 * len(lines) * lines[0].size + 8 * angles * width * length,
            transcendentals=0,
        ),
    )(*operands)


def table_kernel(start_ref, spot_ref, out_ref):
    pair = pl.program_id(0)
    strips, angles, window, cols = out_ref.shape[1:]
    rank = lax.broadcasted_iota(jnp.int32, (window, cols), 0)
    for strip in range(strips):
        for a in range(angles):
            n = strip * angles + a
            place = (rank + start_ref[pair, n] * 128).astype(jnp.float32)
            spot = spot_ref[0, n : n + 1, :]
            out_ref[0, strip, a] = jnp.maximum(0.0, 1.0 - jnp.abs(spot - place)).astype(
                jnp.bfloat16
            )


def make_tables(start, spots, angles):
    pairs, count, cols = spots.shape
    strips = count // angles
    return pl.pallas_call(
        table_kernel,
        name="tables",
        out_shape=jax.ShapeDtypeStruct((pairs, strips, angles, WINDOW, cols), jnp.bfloat16),
        grid_spec=pltpu.PrefetchScalarGridSpec(
            num_scalar_prefetch=1,
            grid=(pairs,),
            in_specs=[pl.BlockSpec((1, count, cols), lambda i, start: (i, 0, 0))],
            out_specs=pl.BlockSpec(
                (1, strips, angles, WINDOW, cols), lambda i, start: (i, 0, 0, 0, 0)
            ),
        ),
        compiler_params=pltpu.CompilerParams(vmem_limit_bytes=48 * MIB),
        cost_estimate=pl.CostEstimate(
            flops=5 * pairs * count * WINDOW * cols,
            bytes_accessed=2 * pairs * count * WINDOW * cols,
            transcendentals=0,
        ),
    )(start, spots)


def back_kernel(start_ref, filt_ref, tables, out_ref, done, out_sem, *, scale):
    pairs, strips, angles, _, cols = tables.shape
    cols = cols // 2
    line = done.shape[1] // (2 * pairs)

    def put(pair):
        across = pl.ds(pl.multiple_of(pair * 2 * line, 2 * line), 2 * line)
        return pltpu.make_async_copy(done.at[:, across], out_ref.at[:, across], out_sem.at[pair])

    def one(step, carry):
        for u in range(4):
            project(step * 4 + u)
        return carry

    def project(pair):
        for strip in range(strips):
            total = None
            for a in range(angles):
                begin = pl.multiple_of(start_ref[pair, strip * angles + a] * 128, 128)
                part = jnp.dot(
                    filt_ref[a, :, pl.ds(begin, WINDOW)],
                    tables[pair, strip, a],
                    preferred_element_type=jnp.float32,
                )
                total = part if total is None else total + part
            total = (total * scale).astype(jnp.bfloat16)
            for r in range(2):
                to = pl.multiple_of(pair * 2 * line + r * line + strip * cols, 128)
                done[:, pl.ds(to, cols)] = total[:, r * cols : (r + 1) * cols]
        put(pair).start()

    lax.fori_loop(0, pairs // 4, one, 0)
    for pair in range(pairs):
        put(pair).wait()


def back_project(start, filt, tables):
    angles, bins, length = filt.shape
    pairs, strips, _, window, cols = tables.shape
    columns = pairs * 2 * length
    return pl.pallas_call(
        functools.partial(back_kernel, scale=math.pi / angles),
        name="back",
        out_shape=jax.ShapeDtypeStruct((bins, columns), jnp.bfloat16),
        in_specs=[
            pl.BlockSpec(memory_space=pltpu.MemorySpace.SMEM),
            pl.BlockSpec(memory_space=VMEM),
            pl.BlockSpec(memory_space=VMEM),
        ],
        out_specs=pl.BlockSpec(memory_space=pl.ANY),
        scratch_shapes=[
            pltpu.VMEM((bins, columns), jnp.bfloat16),
            pltpu.SemaphoreType.DMA((pairs,)),
        ],
        compiler_params=pltpu.CompilerParams(vmem_limit_bytes=24 * MIB),
        cost_estimate=pl.CostEstimate(
            flops=2 * bins * pairs * strips * angles * window * cols,
            bytes_accessed=2 * tables.size + 2 * bins * columns,
            transcendentals=0,
        ),
    )(start, filt, tables)


def shift(array, axis, by):
    pairs = []
    for z in range(SIDE):
        for x in range(SIDE):
            to = (z, (x + by) % SIDE) if axis == "x" else ((z + by) % SIDE, x)
            pairs.append((z * SIDE + x, to[0] * SIDE + to[1]))
    return lax.ppermute(array, "module", pairs)


def swap(array, by, cross):
    pairs = []
    for y in range(SIDE):
        for core in range(2):
            pairs.append((y * 2 + core, (y + by) % SIDE * 2 + (core ^ cross)))
    return lax.ppermute(array, "frame", pairs)


def on_device(frames, weights, monitor, coverage, block_slot, angle_index):
    angles = angle_index.shape[0]
    spots = spot_table(angle_index, ROWS, TRANS)
    spots = spots.reshape(angles, ROWS // 2, 2, TRANS // 128, 128)
    spots = spots.transpose(1, 3, 0, 2, 4).reshape(ROWS // 2, TRANS // 128 * angles, 256)
    start = jnp.floor(jnp.min(spots, axis=2) / 128.0).astype(jnp.int32)
    start = jnp.clip(start, 0, (TRANS - WINDOW) // 128)

    def first_leg(sent):
        halves = [[sent[0]], [sent[SIDE]]]
        for d in FAR:
            for side, axis in enumerate("xz"):
                halves[side].append((d, shift(sent[side * SIDE + d], axis, d)))
        return [[own] + [a for _, a in sorted(rest, key=lambda p: p[0])] for own, *rest in halves]

    def second_leg(halves, relay):
        parts = []
        kept = []
        for side, (axis, other) in enumerate((("x", "z"), ("z", "x"))):
            outs = merge(coverage, halves[side], axis, relay)
            if relay:
                keep0, keep1, keep3, plus, minus = outs
                kept.append((keep0, keep1, keep3, shift(plus, other, 1), shift(minus, other, -1)))
            else:
                parts += [outs[0]] + [shift(outs[e], other, e) for e in (1, 2, 3)]
        for side, other in enumerate("zx"):
            if relay:
                keep0, keep1, keep3, plus, minus = kept[side]
                far_plus = shift(keep1 + plus[0], other, 1)
                far_minus = shift(keep3 + minus[0], other, -1)
                parts += [keep0, plus, minus, far_plus, far_minus]
        own, *others = join(parts, relay)
        return [own] + [swap(o, n // 2, n % 2) for n, o in enumerate(others, 1)]

    begins = [sum(CHUNKS[:c]) for c in range(len(CHUNKS))]
    sent = [
        bin_chunk(block_slot, coverage, frames, weights, monitor, begin, rows, c)
        for c, (begin, rows) in enumerate(zip(begins, CHUNKS))
    ]
    filt = None
    arrived = first_leg(sent[0])
    ramp = ramp_table(TRANS)
    tables = make_tables(start, spots, angles)
    for c, begin in enumerate(begins):
        here = arrived
        last = c + 1 == len(CHUNKS)
        if not last:
            arrived = first_leg(sent[c + 1])
        lines = second_leg(here, RELAY[c])
        filt = ramp_chunk(ramp, lines, filt, begin, last, angles)
    slices = back_project(start, filt, tables)
    return slices.reshape(2, 1, 1, slices.shape[0] // 2, slices.shape[1])


def solution(mesh):
    placed = (
        P("frame", "module"),
        P("module", None, None),
        P("frame"),
        P(),
        P("module", None),
        P(),
    )
    return jax.shard_map(
        on_device,
        mesh=mesh,
        in_specs=placed,
        out_specs=P(None, "frame", "module", None, None),
        check_vma=False,
    )
```

```python
import functools
import math

import jax
import jax.numpy as jnp
from jax import lax
from jax.experimental import pallas as pl
from jax.experimental.pallas import tpu as pltpu
from jax.sharding import PartitionSpec as P

TRANS = 512
ASTEPS = 180
ROWS = 16
NTILE = 256
SIDE = 4
CHUNKS = (160, 96)
RELAY = (False, False)
FAR = (2, 1, 3)
UNROLL = 4
AHEAD = 8
WINDOW = 256

VMEM = pltpu.MemorySpace.VMEM
MIB = 1 << 20
FIRST_MIB = 50


def ramp_table(length):
    places = jnp.arange(length, dtype=jnp.int32)
    offset = places[:, None] - places[None, :]
    is_odd = offset % 2 != 0
    scaled = math.pi * offset.astype(jnp.float32)
    safe_den = jnp.where(is_odd, scaled, jnp.float32(1.0))
    return jnp.where(
        offset == 0,
        jnp.float32(0.25),
        jnp.where(is_odd, -1.0 / (safe_den * safe_den), jnp.float32(0.0)),
    )


def spot_table(angle_index, row_count, length):
    theta_rad = angle_index.astype(jnp.float32) * (math.pi / ASTEPS)
    centre = (length - 1) / 2.0
    across = jnp.arange(length, dtype=jnp.float32) - centre
    down_pos = jnp.arange(row_count, dtype=jnp.float32) - (row_count - 1) / 2.0
    return (
        across[None, None, :] * jnp.cos(theta_rad)[:, None, None]
        + down_pos[None, :, None] * jnp.sin(theta_rad)[:, None, None]
        + centre
    )


def bin_kernel(slot_any, cover_any, mon_any, fr_ref, wt_ref, *rest, begin):
    outs = rest[:-9]
    pixels, tiles, hold, slot_ref, cover_ref, mon_ref, sem, out_sem, small_sem = rest[-9:]
    small = [
        pltpu.make_async_copy(mon_any, mon_ref, small_sem.at[2]),
        pltpu.make_async_copy(slot_any, slot_ref, small_sem.at[0]),
        pltpu.make_async_copy(cover_any, cover_ref, small_sem.at[1]),
    ]
    for copy in small:
        copy.start()
    groups = sem.shape[1]
    depth = pixels.shape[1] // groups
    splits = tiles.shape[0] // groups
    width = tiles.shape[2]
    rows, half = pixels.shape[0], hold.shape[2]
    span = hold.shape[1] // (SIDE * SIDE)

    def fetch(g):
        across = pl.ds(pl.multiple_of(g * depth, depth), depth)
        return (
            pltpu.make_async_copy(
                wt_ref.at[pl.ds(g * splits, splits)],
                tiles.at[pl.ds(g * splits, splits)],
                sem.at[0, g],
            ),
            pltpu.make_async_copy(
                fr_ref.at[pl.ds(begin, rows), across], pixels.at[:, across], sem.at[1, g]
            ),
        )

    for g in range(AHEAD):
        for copy in fetch(g):
            copy.start()
    me = lax.axis_index("module")
    z, x = me // SIDE, me % SIDE
    for copy in small:
        copy.wait()
    flux = mon_ref[0:1, pl.ds(begin, rows)]
    diagonal = lax.broadcasted_iota(jnp.int32, (rows, rows), 0) == lax.broadcasted_iota(
        jnp.int32, (rows, rows), 1
    )
    scale = 1.0 / jnp.sum(jnp.where(diagonal, flux, 0.0), axis=1, keepdims=True)
    first = cover_ref[me, 0]

    def one(turn_pos, carry):
        base = turn_pos * UNROLL
        for u in range(UNROLL):
            for copy in fetch(base + u):
                copy.wait()

        @pl.when(base + AHEAD < groups)
        def _():
            for u in range(UNROLL):
                for copy in fetch(base + AHEAD + u):
                    copy.start()

        for u in range(UNROLL):
            g = base + u
            across = pl.ds(pl.multiple_of(g * depth, depth), depth)
            here = jnp.concatenate([tiles[g * splits + s] for s in range(splits)], axis=1)
            bins = jnp.dot(pixels[:, across], here, preferred_element_type=jnp.float32)
            bins = bins * scale
            for s in range(splits):
                slot = slot_ref[0, g * splits + s]
                owner = (first + slot) & (SIDE * SIDE - 1)
                turn = slot // (SIDE * SIDE)
                away_z = (owner // SIDE - z) & (SIDE - 1)
                away_x = (owner - x) & (SIDE - 1)
                cut = slice(s * width, (s + 1) * width)
                hold[0, (away_x * SIDE + away_z) * span + turn] = bins[:half, cut]
                hold[1, (away_z * SIDE + away_x) * span + turn] = bins[half:, cut]
        return carry

    lax.fori_loop(0, groups // UNROLL, one, 0)
    each = outs[0].shape[0]
    copies = [
        pltpu.make_async_copy(
            hold.at[n // SIDE, pl.ds(n % SIDE * each, each)], out, out_sem.at[n]
        )
        for n, out in enumerate(outs)
    ]
    for copy in copies:
        copy.start()
    for copy in copies:
        copy.wait()


def stay(value):
    return pltpu.with_memory_space_constraint(value, pltpu.MemorySpace.HBM)


def bin_chunk(block_slot, coverage, frames, weights, monitor, begin, rows, tag):
    pixels = frames.shape[1]
    slots, group_pixels, width = weights.shape
    groups = pixels // group_pixels
    half = rows // 2
    each = slots // SIDE
    anywhere = pl.BlockSpec(memory_space=pl.ANY)
    in_hbm = pl.BlockSpec(memory_space=pltpu.MemorySpace.HBM)
    return pl.pallas_call(
        functools.partial(bin_kernel, begin=begin),
        out_shape=[jax.ShapeDtypeStruct((each, half, width), jnp.float32)] * (2 * SIDE),
        in_specs=[in_hbm] * 5,
        out_specs=[in_hbm if n % SIDE == 0 else anywhere for n in range(2 * SIDE)],
        scratch_shapes=[
            pltpu.VMEM((rows, pixels), frames.dtype),
            pltpu.VMEM(weights.shape, weights.dtype),
            pltpu.VMEM((2, slots, half, width), jnp.float32),
            pltpu.SMEM(block_slot.shape, jnp.int32),
            pltpu.SMEM(coverage.shape, jnp.int32),
            pltpu.VMEM((1, monitor.size), monitor.dtype),
            pltpu.SemaphoreType.DMA((2, groups)),
            pltpu.SemaphoreType.DMA((2 * SIDE,)),
            pltpu.SemaphoreType.DMA((3,)),
        ],
        compiler_params=pltpu.CompilerParams(vmem_limit_bytes=(26 if tag else FIRST_MIB) * MIB),
        cost_estimate=pl.CostEstimate(
            flops=2 * rows * pixels * slots // groups * width,
            bytes_accessed=2 * slots * group_pixels * width + 6 * rows * pixels,
            transcendentals=0,
        ),
    )(*(stay(v) for v in (block_slot, coverage, monitor.reshape(1, -1), frames, weights)))


def merge_kernel(cover_ref, *rest, axis, relay):
    sources, outs = rest[:SIDE], rest[SIDE:]
    span = sources[0].shape[0] // SIDE
    modules = SIDE * SIDE
    tiles = NTILE // modules
    half = tiles // 2
    me = lax.axis_index("module")
    z, x = me // SIDE, me % SIDE
    if relay:
        keep0, keep1, keep3, plus, minus = outs
        parts = [
            (2, 0, plus.at[0]),
            (2, 1, minus.at[0]),
            (1, 0, keep1),
            (1, 1, plus.at[1]),
            (3, 0, minus.at[1]),
            (3, 1, keep3),
            (0, 0, keep0.at[pl.ds(0, half)]),
            (0, 1, keep0.at[pl.ds(half, half)]),
        ]
    else:
        parts = [(e, p, outs[e].at[pl.ds(p * half, half)]) for e in range(SIDE) for p in range(2)]
    for e, part, out in parts:
        begin = []
        for d in range(SIDE):
            if axis == "x":
                source = z * SIDE + ((x - d) & (SIDE - 1))
                owner = ((z + e) & (SIDE - 1)) * SIDE + x
            else:
                source = ((z - d) & (SIDE - 1)) * SIDE + x
                owner = z * SIDE + ((x + e) & (SIDE - 1))
            first = cover_ref[source, 0]
            skip = (owner - first) & (modules - 1)
            begin.append(((first + skip) // modules) & (tiles - 1))

        def one(k, carry, e=e, part=part, begin=begin, out=out):
            total = None
            for d in range(SIDE):
                j = (k + part * half - begin[d]) & (tiles - 1)
                tile = sources[d][e * span + jnp.minimum(j, span - 1)]
                tile = jnp.where(j < span, tile, 0.0)
                total = tile if total is None else total + tile
            out[k] = total
            return carry

        lax.fori_loop(0, half, one, 0)


def merge(coverage, sources, axis, relay):
    each, rows, width = sources[0].shape
    tiles = NTILE // (SIDE * SIDE)
    half = tiles // 2

    def shape(*lead):
        return jax.ShapeDtypeStruct((*lead, rows, width), jnp.float32)

    if relay:
        outs = [shape(tiles), shape(half), shape(half), shape(2, half), shape(2, half)]
    else:
        outs = [shape(tiles)] * SIDE
    return pl.pallas_call(
        functools.partial(merge_kernel, axis=axis, relay=relay),
        out_shape=outs,
        in_specs=[pl.BlockSpec(memory_space=pltpu.MemorySpace.SMEM)]
        + [pl.BlockSpec(memory_space=VMEM)] * SIDE,
        out_specs=[pl.BlockSpec(memory_space=VMEM)] * len(outs),
        compiler_params=pltpu.CompilerParams(vmem_limit_bytes=14 * MIB),
        cost_estimate=pl.CostEstimate(
            flops=4 * 64 * rows * width,
            bytes_accessed=4 * rows * width * (4 * each + 64),
            transcendentals=0,
        ),
    )(coverage, *sources)


def join_kernel(*refs, relay):
    count = 5 if relay else 4
    outs = refs[2 * count :]
    me = lax.axis_index("frame")
    y, core = me // 2, me % 2
    half = refs[0].shape[0] // 2
    for n, out in enumerate(outs):
        owner = ((y + n // 2) & (SIDE - 1)) * 2 + (core ^ (n % 2))
        for side in range(2):
            parts = refs[count * side : count * (side + 1)]
            if relay:
                keep0, plus, minus, far_plus, far_minus = parts
                out[side] = keep0[owner] + minus[1, owner] + far_plus[owner]
                out[2 + side] = keep0[half + owner] + plus[1, owner] + far_minus[owner]
            else:
                for q in range(2):
                    k = q * half + owner
                    out[2 * q + side] = parts[0][k] + parts[1][k] + (parts[2][k] + parts[3][k])


def join(parts, relay):
    tiles, rows, width = parts[0].shape
    half = tiles // 2
    return pl.pallas_call(
        functools.partial(join_kernel, relay=relay),
        out_shape=[jax.ShapeDtypeStruct((4, rows, width), jnp.float32)] * half,
        in_specs=[pl.BlockSpec(memory_space=VMEM)] * len(parts),
        out_specs=[pl.BlockSpec(memory_space=VMEM)] * half,
        compiler_params=pltpu.CompilerParams(vmem_limit_bytes=14 * MIB),
        cost_estimate=pl.CostEstimate(
            flops=8 * half * rows * width,
            bytes_accessed=4 * rows * width * half * 18,
            transcendentals=0,
        ),
    )(*parts)


def split(value):
    high = value.astype(jnp.bfloat16)
    return high, (value - high.astype(jnp.float32)).astype(jnp.bfloat16)


def filter_kernel(ramp_ref, *rest, begin, count):
    lines, out = rest[:count], rest[-1]
    prev = rest[count] if len(rest) == count + 2 else None
    rows = 2 * lines[0].shape[1]
    width = lines[0].shape[2]
    me = lax.axis_index("frame")
    y, core = me // 2, me % 2
    per_group = ramp_ref.shape[0] // 2
    ramp = jnp.concatenate(
        [ramp_ref[pl.ds((core ^ dc) * per_group + begin, rows), :] for dc in range(2)], axis=0
    )
    ramp_high, ramp_low = split(ramp)
    for dy in range(SIDE):
        a = (y - dy) & (SIDE - 1)
        for q in range(2):
            both = [
                lines[2 * dy + dc][2 * q : 2 * q + 2].reshape(rows, width) for dc in range(2)
            ]
            high, low = split(jnp.concatenate(both, axis=0).T)
            total = jnp.dot(high, ramp_high, preferred_element_type=jnp.float32)
            total = total + jnp.dot(high, ramp_low, preferred_element_type=jnp.float32)
            total = total + jnp.dot(low, ramp_high, preferred_element_type=jnp.float32)
            here = slice(q * width, (q + 1) * width)
            if prev is not None:
                total = total + prev[a, here]
            out[a, here] = total.astype(out.dtype)


def ramp_chunk(ramp, lines, prev, begin, last, angles):
    width = lines[0].shape[2]
    length = ramp.shape[0]
    operands = [ramp, *lines] + ([] if prev is None else [prev])
    return pl.pallas_call(
        functools.partial(filter_kernel, begin=begin, count=len(lines)),
        out_shape=jax.ShapeDtypeStruct(
            (angles, 2 * width, length), jnp.bfloat16 if last else jnp.float32
        ),
        in_specs=[pl.BlockSpec(memory_space=VMEM)] * len(operands),
        out_specs=pl.BlockSpec(memory_space=VMEM),
        compiler_params=pltpu.CompilerParams(vmem_limit_bytes=14 * MIB),
        cost_estimate=pl.CostEstimate(
            flops=6 * angles * 2 * width * length * length // 2,
            bytes_accessed=4 * len(lines) * lines[0].size + 8 * angles * width * length,
            transcendentals=0,
        ),
    )(*operands)


def table_kernel(start_ref, spot_ref, out_ref):
    pair = pl.program_id(0)
    strips, angles, window, cols = out_ref.shape[1:]
    rank = lax.broadcasted_iota(jnp.int32, (window, cols), 0)
    for strip in range(strips):
        for a in range(angles):
            n = strip * angles + a
            place = (rank + start_ref[pair, n] * 128).astype(jnp.float32)
            spot = spot_ref[0, n : n + 1, :]
            out_ref[0, strip, a] = jnp.maximum(0.0, 1.0 - jnp.abs(spot - place)).astype(
                jnp.bfloat16
            )


def make_tables(start, spots, angles):
    pairs, count, cols = spots.shape
    strips = count // angles
    return pl.pallas_call(
        table_kernel,
        name="tables",
        out_shape=jax.ShapeDtypeStruct((pairs, strips, angles, WINDOW, cols), jnp.bfloat16),
        grid_spec=pltpu.PrefetchScalarGridSpec(
            num_scalar_prefetch=1,
            grid=(pairs,),
            in_specs=[pl.BlockSpec((1, count, cols), lambda i, start: (i, 0, 0))],
            out_specs=pl.BlockSpec(
                (1, strips, angles, WINDOW, cols), lambda i, start: (i, 0, 0, 0, 0)
            ),
        ),
        compiler_params=pltpu.CompilerParams(vmem_limit_bytes=40 * MIB),
        cost_estimate=pl.CostEstimate(
            flops=5 * pairs * count * WINDOW * cols,
            bytes_accessed=2 * pairs * count * WINDOW * cols,
            transcendentals=0,
        ),
    )(start, spots)


def back_kernel(start_ref, filt_ref, tables, out_ref, done, out_sem, *, scale):
    pairs, strips, angles, _, cols = tables.shape
    cols = cols // 2
    line = done.shape[1] // (2 * pairs)

    def put(pair):
        across = pl.ds(pl.multiple_of(pair * 2 * line, 2 * line), 2 * line)
        return pltpu.make_async_copy(done.at[:, across], out_ref.at[:, across], out_sem.at[pair])

    def one(step, carry):
        for u in range(4):
            project(step * 4 + u)
        return carry

    def project(pair):
        for strip in range(strips):
            total = None
            for a in range(angles):
                begin = pl.multiple_of(start_ref[pair, strip * angles + a] * 128, 128)
                part = jnp.dot(
                    filt_ref[a, :, pl.ds(begin, WINDOW)],
                    tables[pair, strip, a],
                    preferred_element_type=jnp.float32,
                )
                total = part if total is None else total + part
            total = (total * scale).astype(jnp.bfloat16)
            for r in range(2):
                to = pl.multiple_of(pair * 2 * line + r * line + strip * cols, 128)
                done[:, pl.ds(to, cols)] = total[:, r * cols : (r + 1) * cols]
        put(pair).start()

    lax.fori_loop(0, pairs // 4, one, 0)
    for pair in range(pairs):
        put(pair).wait()


def back_project(start, filt, tables):
    angles, bins, length = filt.shape
    pairs, strips, _, window, cols = tables.shape
    columns = pairs * 2 * length
    return pl.pallas_call(
        functools.partial(back_kernel, scale=math.pi / angles),
        name="back",
        out_shape=jax.ShapeDtypeStruct((bins, columns), jnp.bfloat16),
        in_specs=[
            pl.BlockSpec(memory_space=pltpu.MemorySpace.SMEM),
            pl.BlockSpec(memory_space=VMEM),
            pl.BlockSpec(memory_space=VMEM),
        ],
        out_specs=pl.BlockSpec(memory_space=pl.ANY),
        scratch_shapes=[
            pltpu.VMEM((bins, columns), jnp.bfloat16),
            pltpu.SemaphoreType.DMA((pairs,)),
        ],
        compiler_params=pltpu.CompilerParams(vmem_limit_bytes=24 * MIB),
        cost_estimate=pl.CostEstimate(
            flops=2 * bins * pairs * strips * angles * window * cols,
            bytes_accessed=2 * tables.size + 2 * bins * columns,
            transcendentals=0,
        ),
    )(start, filt, tables)


def shift(array, axis, by):
    pairs = []
    for z in range(SIDE):
        for x in range(SIDE):
            to = (z, (x + by) % SIDE) if axis == "x" else ((z + by) % SIDE, x)
            pairs.append((z * SIDE + x, to[0] * SIDE + to[1]))
    return lax.ppermute(array, "module", pairs)


def swap(array, by, cross):
    pairs = []
    for y in range(SIDE):
        for core in range(2):
            pairs.append((y * 2 + core, (y + by) % SIDE * 2 + (core ^ cross)))
    return lax.ppermute(array, "frame", pairs)


def on_device(frames, weights, monitor, coverage, block_slot, angle_index):
    angles = angle_index.shape[0]
    spots = spot_table(angle_index, ROWS, TRANS)
    spots = spots.reshape(angles, ROWS // 2, 2, TRANS // 128, 128)
    spots = spots.transpose(1, 3, 0, 2, 4).reshape(ROWS // 2, TRANS // 128 * angles, 256)
    start = jnp.floor(jnp.min(spots, axis=2) / 128.0).astype(jnp.int32)
    start = jnp.clip(start, 0, (TRANS - WINDOW) // 128)

    def first_leg(sent):
        halves = [[sent[0]], [sent[SIDE]]]
        for d in FAR:
            for side, axis in enumerate("xz"):
                halves[side].append((d, shift(sent[side * SIDE + d], axis, d)))
        return [[own] + [a for _, a in sorted(rest, key=lambda p: p[0])] for own, *rest in halves]

    def second_leg(halves, relay):
        parts = []
        kept = []
        for side, (axis, other) in enumerate((("x", "z"), ("z", "x"))):
            outs = merge(coverage, halves[side], axis, relay)
            if relay:
                keep0, keep1, keep3, plus, minus = outs
                kept.append((keep0, keep1, keep3, shift(plus, other, 1), shift(minus, other, -1)))
            else:
                parts += [outs[0]] + [shift(outs[e], other, e) for e in (1, 2, 3)]
        for side, other in enumerate("zx"):
            if relay:
                keep0, keep1, keep3, plus, minus = kept[side]
                far_plus = shift(keep1 + plus[0], other, 1)
                far_minus = shift(keep3 + minus[0], other, -1)
                parts += [keep0, plus, minus, far_plus, far_minus]
        own, *others = join(parts, relay)
        return [own] + [swap(o, n // 2, n % 2) for n, o in enumerate(others, 1)]

    begins = [sum(CHUNKS[:c]) for c in range(len(CHUNKS))]
    sent = [
        bin_chunk(block_slot, coverage, frames, weights, monitor, begin, rows, c)
        for c, (begin, rows) in enumerate(zip(begins, CHUNKS))
    ]
    filt = None
    arrived = first_leg(sent[0])
    ramp = ramp_table(TRANS)
    tables = make_tables(start, spots, angles)
    for c, begin in enumerate(begins):
        here = arrived
        last = c + 1 == len(CHUNKS)
        if not last:
            arrived = first_leg(sent[c + 1])
        lines = second_leg(here, RELAY[c])
        filt = ramp_chunk(ramp, lines, filt, begin, last, angles)
    slices = back_project(start, filt, tables)
    return slices.reshape(2, 1, 1, slices.shape[0] // 2, slices.shape[1])


def solution(mesh):
    placed = (
        P("frame", "module"),
        P("module", None, None),
        P("frame"),
        P(),
        P("module", None),
        P(),
    )
    return jax.shard_map(
        on_device,
        mesh=mesh,
        in_specs=placed,
        out_specs=P(None, "frame", "module", None, None),
        check_vma=False,
    )
```
